128 devices in a mesh: lon: 32 (over y_hi, z, x), lat: 4 (over y_lo, core).
Axes of the slice: x: 4, y: 4 (y_hi: 2, y_lo: 2; y = y_hi * 2 + y_lo), z: 4, core: 2. Of those that a mesh axis runs over, the one named last changes fastest.
Arguments:
- state: float32 [25, 512, 4096], P(None, 'lat', 'lon'), may hold values from -6 to 6
- adjoint_in: float32 [25, 512, 4096], P(None, 'lat', 'lon'), may hold values from -6 to 6
- land_mask: int32 [512, 4096], P('lat', 'lon'), may hold values 0 or 1
- east_coef: float32 [512, 4096], P('lat', 'lon'), may hold values from 0.03 to 0.25
- north_coef: float32 [512, 4096], P('lat', 'lon'), may hold values from 0.03 to 0.25
- zonal_flow: float32 [512, 4096], P('lat', 'lon'), may hold values from -0.2 to 0.2
- vertical_coef: float32 [512, 4096], P('lat', 'lon'), may hold values from 0.05 to 0.3
- slot_cell: int32 [128, 8192], P(('lon', 'lat')), may hold values from -1 to 16383, as said below
- slot_weight: float32 [128, 8192], P(('lon', 'lat')), may hold values from 0.1 to 1
- arrive_obs: int32 [128, 8192], P(('lon', 'lat')), may hold values from -1 to 511, as said below
- obs_value: float32 [25, 65536], P(None, ('lon', 'lat')), may hold values from -6 to 6
- obs_invvar: float32 [25, 65536], P(None, ('lon', 'lat')), may hold values from 0.5 to 4
Outputs:
- adjoint_state: float32 [25, 512, 4096], P(None, 'lat', 'lon')
- misfit: float32 [25, 65536], P(None, ('lon', 'lat'))
The draws below stay inside these ranges and needn't reach their ends.
Inputs may be any that keep to these rules, and one draw needn't show every extreme that they name: slot_cell[s, t * 64 + p] is the index, row-major over the 128 x 128 block of device s, of the cell that slot p from device s to device t reads, or -1 where that slot is empty; from each device to each device the live slots are those with p below a count of 1 to 64, and some device receives 64 live slots from every device. arrive_obs[t, s * 64 + p] is the observation of device t fed by slot p from device s, and is -1 exactly where slot_cell[s, t * 64 + p] is -1.
All inputs are finite; a program needn't handle non-finite values. No bound on the sum of `land_mask` on one device may be relied on, other than what follows from the above.
Results may differ from the reference program's by a relative error of at most 0.00002.
Values sent between devices are 32-bit elements; how exact they have to be, the bound alone decides.
A program may use at most 64 MiB of HBM per device.

```python
import math
import jax
import jax.numpy as jnp

LEVELS = 25
STEPS = 2
CLAT = 128
CLON = 128
CAP = 64
OBS_DEV = 512
NLAT = 512
NLON = 4096
CELLS = 16384
SLOTS = 8192
NOBS = 65536
N_LON = 32
N_LAT = 4
DEVICES = 128


def slot_plan(key):
    base_key = jax.random.fold_in(key, 11)
    keys = jax.random.split(base_key, 4)
    counts = jax.random.randint(keys[0], (DEVICES, DEVICES), 1, CAP + 1)
    full_owner = jax.random.randint(keys[1], (), 0, DEVICES)
    counts = jnp.where(jnp.arange(DEVICES)[None, :] == full_owner, CAP, counts)
    live_slot = jnp.arange(CAP)[None, None, :] < counts[:, :, None]
    cell_draw = jax.random.randint(keys[2], (DEVICES, DEVICES, CAP), 0, CLAT * CLON)
    target_draw = jax.random.randint(keys[3], (DEVICES, DEVICES, CAP), 0, OBS_DEV)
    return (live_slot, cell_draw, target_draw)


def draw_slot_cell(key, part):
    live_slot, cell_draw, target_draw = slot_plan(key)
    return jnp.where(live_slot, cell_draw, -1).reshape(DEVICES, DEVICES * CAP).astype(jnp.int32)


def draw_arrive_obs(key, part):
    live_slot, cell_draw, target_draw = slot_plan(key)
    marked = jnp.where(live_slot, target_draw, -1)
    return marked.transpose(1, 0, 2).reshape(DEVICES, DEVICES * CAP).astype(jnp.int32)


def plant(entries, own_key, low, largest):
    extent = entries.shape
    index_at = [jax.random.randint(jax.random.fold_in(own_key, axis), (), 0, extent[axis]) for axis in range(len(extent))]
    entries = entries.at[tuple(index_at)].set(low)
    longest = extent.index(max(extent))
    index_at[longest] = (index_at[longest] + 1) % extent[longest]
    return entries.at[tuple(index_at)].set(largest)


def level_of(own_key, shape, pieces, low, largest):
    def one(position, parts):
        draws = jax.random.uniform(jax.random.fold_in(jax.random.fold_in(own_key, 6), position), (parts,), jnp.float32, low / len(pieces), largest / len(pieces))
        return jnp.repeat(jnp.exp(draws), shape[position] // parts).reshape((-1,) + (1,) * (len(shape) - position - 1))

    gain = one(*pieces[0])
    for cut in pieces[1:]:
        gain = gain * one(*cut)
    return gain


def gaussian(stream_key, dims, scale, bound, shards=(), dtype=jnp.bfloat16):
    values = scale * jax.random.normal(stream_key, dims, jnp.float32)
    if shards:
        values = values * level_of(stream_key, dims, shards, -0.22, 0.18)
    return jnp.clip(values, -bound, bound).astype(dtype)


def setup_inputs(seed: int = 0) -> dict:
    splits = jax.random.split(jax.random.key(seed), 13)
    return {
        "state": gaussian(splits[0], (LEVELS, NLAT, NLON), 1.0, 6.0, ((1, 4), (2, 32)), jnp.float32),
        "adjoint_in": gaussian(splits[1], (LEVELS, NLAT, NLON), 1.0, 6.0, ((1, 4), (2, 32)), jnp.float32),
        "land_mask": plant((jax.random.randint(splits[2], (NLAT, NLON), 0, 4) < 3).astype(jnp.int32), jax.random.fold_in(splits[2], 1), 0, 1),
        "east_coef": jnp.clip(jnp.exp(math.log(0.25) - 2.1202636 * jax.random.uniform(splits[3], (NLAT, NLON), jnp.float32) ** level_of(splits[3], (NLAT, NLON), ((0, 4), (1, 32)), -0.2, 0.2)), 0.03, 0.25),
        "north_coef": jnp.clip(jnp.exp(math.log(0.25) - 2.1202636 * jax.random.uniform(splits[4], (NLAT, NLON), jnp.float32) ** level_of(splits[4], (NLAT, NLON), ((0, 4), (1, 32)), -0.2, 0.2)), 0.03, 0.25),
        "zonal_flow": jnp.clip(jax.random.uniform(splits[5], (NLAT, NLON), jnp.float32, -0.2, 0.2) * level_of(splits[5], (NLAT, NLON), ((0, 4), (1, 32)), -0.4, 0.0), -0.2, 0.2),
        "vertical_coef": jnp.clip(jnp.exp(math.log(0.3) - 1.7917595 * jax.random.uniform(splits[6], (NLAT, NLON), jnp.float32) ** level_of(splits[6], (NLAT, NLON), ((0, 4), (1, 32)), -0.2, 0.2)), 0.05, 0.3),
        "slot_cell": draw_slot_cell(jax.random.fold_in(splits[12], 71), 0),
        "slot_weight": jnp.clip(0.1 + 0.9 * jax.random.uniform(splits[8], (DEVICES, SLOTS), jnp.float32) ** level_of(splits[8], (DEVICES, SLOTS), ((0, 128),), -0.2, 0.2), 0.1, 1.0),
        "arrive_obs": draw_arrive_obs(jax.random.fold_in(splits[12], 71), 0),
        "obs_value": gaussian(splits[10], (LEVELS, NOBS), 1.0, 6.0, ((1, 128),), jnp.float32),
        "obs_invvar": jnp.clip(jnp.exp(math.log(4.0) - 2.0794415 * jax.random.uniform(splits[11], (LEVELS, NOBS), jnp.float32) ** level_of(splits[11], (LEVELS, NOBS), ((1, 128),), -0.2, 0.2)), 0.5, 4.0),
    }


def to_blocks(field):
    return field.reshape(LEVELS, N_LAT, CLAT, N_LON, CLON).transpose(0, 3, 1, 2, 4).reshape(LEVELS, DEVICES, CELLS)

def from_blocks(blocked):
    return blocked.reshape(LEVELS, N_LON, N_LAT, CLAT, CLON).transpose(0, 2, 3, 1, 4).reshape(LEVELS, NLAT, NLON)

def model_step(field, ocean, east_coef, north_coef, zonal_flow, vertical_coef):
    east_field = jnp.roll(field, -1, axis=2)
    north_field = jnp.concatenate([field[:, 1:, :], field[:, -1:, ::-1]], axis=1)
    east_flux = east_coef * (east_field - field) - 0.5 * zonal_flow * (field + east_field)
    north_flux = north_coef * (north_field - field)
    zero_row = jnp.zeros_like(north_flux[:, :1, :])
    divergence = east_flux - jnp.roll(east_flux, 1, axis=2)
    divergence = divergence + north_flux - jnp.concatenate([zero_row, north_flux[:, :-1, :]], axis=1)
    vertical_flux = vertical_coef * (field[1:] - field[:-1])
    zero_level = jnp.zeros_like(field[:1])
    divergence = divergence + jnp.concatenate([vertical_flux, zero_level], axis=0)
    divergence = divergence - jnp.concatenate([zero_level, vertical_flux], axis=0)
    return field + ocean * divergence

def reference(state, adjoint_in, land_mask, east_coef, north_coef, zonal_flow, vertical_coef, slot_cell, slot_weight, arrive_obs, obs_value, obs_invvar):
    blocked = to_blocks(state)
    live_slot = slot_cell >= 0
    cell_index = jnp.where(live_slot, slot_cell, 0).astype(jnp.int32)
    weights = jnp.where(live_slot, slot_weight, jnp.zeros_like(slot_weight))
    picked = jnp.take_along_axis(blocked, cell_index[None], axis=2)
    partial_vals = picked * weights[None]
    at_owner = partial_vals.reshape(LEVELS, DEVICES, DEVICES, CAP).transpose(0, 2, 1, 3).reshape(LEVELS, DEVICES, SLOTS)
    live_target = arrive_obs >= 0
    owner_base = (jnp.arange(DEVICES).astype(jnp.int32) * OBS_DEV)[:, None]
    global_id = jnp.where(live_target, owner_base + arrive_obs, NOBS).astype(jnp.int32)
    interp = jnp.zeros((LEVELS, NOBS + 1), jnp.float32).at[:, global_id.reshape(-1)].add(at_owner.reshape(LEVELS, -1))[:, :NOBS]
    misfit = obs_invvar * (interp - obs_value)
    clipped = jnp.minimum(global_id, NOBS - 1).astype(jnp.int32)
    returned = jnp.where(live_target[None], misfit[:, clipped], jnp.zeros((), jnp.float32))
    returned = returned.reshape(LEVELS, DEVICES, DEVICES, CAP).transpose(0, 2, 1, 3).reshape(LEVELS, DEVICES, SLOTS)
    weighted = returned * weights[None]
    cell_base = (jnp.arange(DEVICES).astype(jnp.int32) * CELLS)[:, None]
    cell_id = jnp.where(live_slot, cell_base + slot_cell, DEVICES * CELLS).astype(jnp.int32)
    forcing = jnp.zeros((LEVELS, DEVICES * CELLS + 1), jnp.float32).at[:, cell_id.reshape(-1)].add(weighted.reshape(LEVELS, -1))
    forcing = forcing[:, :DEVICES * CELLS].reshape(LEVELS, DEVICES, CELLS)
    adjoint_seed = adjoint_in + from_blocks(forcing)
    ocean = land_mask.astype(jnp.float32)

    def advance(field):
        return model_step(field, ocean, east_coef, north_coef, zonal_flow, vertical_coef)
    unused, pull_back = jax.vjp(advance, state)
    adjoint_state = adjoint_seed
    for repeat in range(STEPS):
        adjoint_state = pull_back(adjoint_state)[0]
    return (adjoint_state, misfit)
```

```python
import jax
import jax.numpy as jnp
from jax import lax
from jax.sharding import PartitionSpec as P

STEPS = 2


def from_behind(value, axis, steps):
    count = lax.axis_size(axis)
    pairs = [(source, (source + steps) % count) for source in range(count)]
    return lax.ppermute(value, axis, pairs)


def from_behind_2(block, axis, distance):
    devices = range(lax.axis_size(axis))
    route = [(i - distance, i) for i in devices if i - distance in devices]
    return lax.ppermute(block, axis, route)


def padded(cells, sides, width, closed):
    for axis, dim in sides:
        count = lax.axis_size(axis)
        ends = count if closed else count - 1
        head = lax.slice_in_dim(cells, 0, width, axis=dim)
        tail = lax.slice_in_dim(cells, cells.shape[dim] - width, cells.shape[dim], axis=dim)
        cells = jnp.concatenate(
            [
                lax.ppermute(tail, axis, [(i, (i + 1) % count) for i in range(ends)]),
                cells,
                lax.ppermute(head, axis, [((i + 1) % count, i) for i in range(ends)]),
            ],
            axis=dim,
        )
    return cells


def on_device(
    state,
    adjoint_in,
    land_mask,
    east_coef,
    north_coef,
    zonal_flow,
    vertical_coef,
    slot_cell,
    slot_weight,
    arrive_obs,
    obs_value,
    obs_invvar,
):
    levels_n, rows_n, cols_n = state.shape
    flat_state = state.reshape(levels_n, rows_n * cols_n)
    slot_row = slot_cell[0]
    live_slot = slot_row >= 0
    cell_index = jnp.where(live_slot, slot_row, 0)
    weights = jnp.where(live_slot, slot_weight[0], 0.0)
    partial_vals = flat_state[:, cell_index] * weights[None, :]
    arrived = lax.all_to_all(partial_vals, ("lon", "lat"), split_axis=1, concat_axis=1, tiled=True)
    target_row = arrive_obs[0]
    live_target = target_row >= 0
    target_index = jnp.where(live_target, target_row, 0)
    incoming = jnp.where(live_target[None, :], arrived, 0.0)
    interp = jnp.zeros(obs_value.shape, jnp.float32).at[:, target_index].add(incoming)
    misfit = obs_invvar * (interp - obs_value)
    outgoing = jnp.where(live_target[None, :], misfit[:, target_index], 0.0)
    returned = lax.all_to_all(outgoing, ("lon", "lat"), split_axis=1, concat_axis=1, tiled=True)
    forcing = (
        jnp.zeros((levels_n, rows_n * cols_n), jnp.float32)
        .at[:, cell_index]
        .add(returned * weights[None, :])
    )
    adjoint_state = adjoint_in + forcing.reshape(state.shape)
    ocean = land_mask.astype(jnp.float32)
    east_weight = east_coef - 0.5 * zonal_flow
    own_east = east_coef + 0.5 * zonal_flow
    west_column = from_behind(east_weight[:, -1:], "lon", 1)
    west_weight = jnp.concatenate([west_column, east_weight[:, :-1]], axis=1)
    south_row = from_behind_2(north_coef[-1:, :], "lat", 1)
    south_weight = jnp.concatenate([south_row, north_coef[:-1, :]], axis=0)
    lat_last = lax.axis_index("lat") == lax.axis_size("lat") - 1
    zero_level = jnp.zeros((1, rows_n, cols_n), jnp.float32)
    for repeat in range(STEPS):
        masked = ocean * adjoint_state
        zonal_pad = padded(masked, (("lon", 2),), 1, True)
        merid_pad = padded(masked, (("lat", 1),), 1, False)
        east_vals = zonal_pad[:, :, 2:]
        west_vals = zonal_pad[:, :, :-2]
        north_vals = merid_pad[:, 2:, :]
        south_vals = merid_pad[:, :-2, :]
        east_diff = masked - east_vals
        north_diff = masked - north_vals
        updated = adjoint_state - own_east * east_diff + west_weight * (west_vals - masked)
        updated = updated - north_coef * north_diff + south_weight * (south_vals - masked)
        fold_top = north_coef[-1][None, :] * masked[:, -1, :]
        lon_n = lax.axis_size("lon")
        mirror = [(i, lon_n - 1 - i) for i in range(lon_n)]
        mirrored = lax.ppermute(fold_top[:, ::-1], "lon", mirror)
        updated = updated.at[:, -1, :].add(jnp.where(lat_last, mirrored, 0.0))
        vertical_term = vertical_coef[None] * (masked[:-1] - masked[1:])
        updated = updated - jnp.concatenate([vertical_term, zero_level], axis=0)
        updated = updated + jnp.concatenate([zero_level, vertical_term], axis=0)
        adjoint_state = updated
    return (adjoint_state, misfit)


def solution(mesh):
    in_specs = (
        P(None, "lat", "lon"),
        P(None, "lat", "lon"),
        P("lat", "lon"),
        P("lat", "lon"),
        P("lat", "lon"),
        P("lat", "lon"),
        P("lat", "lon"),
        P(("lon", "lat"), None),
        P(("lon", "lat"), None),
        P(("lon", "lat"), None),
        P(None, ("lon", "lat")),
        P(None, ("lon", "lat")),
    )
    out_specs = (P(None, "lat", "lon"), P(None, ("lon", "lat")))
    return jax.shard_map(
        on_device, mesh=mesh, in_specs=in_specs, out_specs=out_specs, check_vma=False
    )
```

```python
import functools
import jax, jax.numpy as jnp
from jax import lax
from jax.experimental import pallas as pl
from jax.experimental.pallas import tpu as pltpu
VM=pl.BlockSpec(memory_space=pltpu.VMEM)
BF=jnp.bfloat16; F32=jnp.float32

def cparts(cell):
    row=lax.bitwise_and(lax.shift_right_arithmetic(cell,7),63)
    col=lax.bitwise_or(lax.shift_left(lax.shift_right_arithmetic(cell,13),7),lax.bitwise_and(cell,127))
    return row,col

def split_state(st, hi, lo):
    for half in range(2):
        v=st[:, half*64:(half+1)*64, :].reshape(1600,128)
        h=v.astype(BF)
        hi[:, half*128:(half+1)*128]=h
        lo[:, half*128:(half+1)*128]=(v-h.astype(F32)).astype(BF)

def gk(cell_ref,w_ref,st,out,hi,lo,*b):
    split_state(st,hi,lo)
    lane=lax.broadcasted_iota(jnp.int32,(13,256),1)
    low=lax.bitwise_and(lane,127)<64
    def chunk(a,_):
        o=pl.multiple_of(a*256,256)
        cell=cell_ref[:,pl.ds(o,256)]
        w=jnp.where(cell>=0,w_ref[:,pl.ds(o,256)],0.0)
        row,col=cparts(cell)
        C=(lax.broadcasted_iota(jnp.int32,(256,256),0)==col).astype(F32).astype(BF)
        R=jnp.where(lax.broadcasted_iota(jnp.int32,(64,256),0)==row,w,0.0)
        LG=5
        for g in range(5):
            r0=g*LG*64
            T=jnp.dot(hi[r0:r0+LG*64,:],C,preferred_element_type=F32)+jnp.dot(lo[r0:r0+LG*64,:],C,preferred_element_type=F32)
            T=T.reshape(LG,8,8,256)*R.reshape(1,8,8,256)
            T=jnp.sum(T,axis=1).reshape(LG*8,256)
            for q in range(2):
                b[q][pl.ds(g*LG*8,LG*8),:]=T[:,q*128:(q+1)*128]
        def gather(b,r0):
            x=b[pl.ds(r0*8,13,stride=8),:]
            for s in range(1,8):
                x=x+b[pl.ds(r0*8+s,13,stride=8),:]
            return x
        for q in range(2):
            va=gather(b[q],0); vb=gather(b[q],13)
            lw=low[:,:128]
            out[a*4+2*q,0:13,:]=jnp.where(lw,va,pltpu.roll(vb,64,1))
            out[a*4+2*q+1,0:13,:]=jnp.where(lw,pltpu.roll(va,64,1),vb)
        return 0
    lax.fori_loop(0,32,chunk,0)

def gather(state,cell,w):
    return pl.pallas_call(gk,out_shape=jax.ShapeDtypeStruct((128,16,128),F32),in_specs=[VM]*3,out_specs=VM,
        scratch_shapes=[pltpu.VMEM((1600,256),BF)]*2+[pltpu.VMEM((208,128),F32)]*2,
        compiler_params=pltpu.CompilerParams(vmem_limit_bytes=60<<20),name="gk")(cell,w,state)

def sk(cell_ref,w_ref,adj,ret,out,F,A):
    for half in range(2):
        F[:,half*128:(half+1)*128]=adj[:,half*64:(half+1)*64,:].reshape(1600,128)
    lane=lax.broadcasted_iota(jnp.int32,(16,128),1)
    lw=lane<64
    def chunk(a,_):
        o=pl.multiple_of(a*256,256)
        cell=cell_ref[:,pl.ds(o,256)]
        w=jnp.where(cell>=0,w_ref[:,pl.ds(o,256)],0.0)
        row,col=cparts(cell)
        Ct=(lax.broadcasted_iota(jnp.int32,(256,256),0)==col).astype(F32).astype(BF)
        R=(lax.broadcasted_iota(jnp.int32,(64,256),0)==row).astype(F32).astype(BF)
        xa=[];xb=[]
        for q in range(2):
            m0=ret[a*4+2*q]; m1=ret[a*4+2*q+1]
            xa.append(jnp.where(lw,m0,pltpu.roll(m1,64,1)))
            xb.append(jnp.where(lw,pltpu.roll(m0,64,1),m1))
        xa=jnp.concatenate(xa,1)*w; xb=jnp.concatenate(xb,1)*w
        xah=xa.astype(BF).astype(F32); xal=xa-xah
        xbh=xb.astype(BF).astype(F32); xbl=xb-xbh
        for l in range(25):
            x,j=(xah,l) if l<13 else (xbh,l-13)
            y=(xal if l<13 else xbl)
            A[l*64:(l+1)*64,0:256]=R*jnp.broadcast_to(x[j:j+1],(64,256)).astype(BF)
            A[l*64:(l+1)*64,256:512]=R*jnp.broadcast_to(y[j:j+1],(64,256)).astype(BF)
        dn=(((1,),(1,)),((),()))
        CC=jnp.concatenate([Ct,Ct],1)
        for g in range(5):
            sl=slice(g*320,(g+1)*320)
            F[sl,:]+=lax.dot_general(A[sl,:],CC,dn,preferred_element_type=F32)
        return 0
    lax.fori_loop(0,32,chunk,0)
    for half in range(2):
        out[:,half*64:(half+1)*64,:]=F[:,half*128:(half+1)*128].reshape(25,64,128)

def scatter(adj,ret,cell,w):
    return pl.pallas_call(sk,out_shape=jax.ShapeDtypeStruct((25,128,128),F32),in_specs=[VM]*4,out_specs=VM,
        scratch_shapes=[pltpu.VMEM((1600,256),F32),pltpu.VMEM((1600,512),BF)],
        compiler_params=pltpu.CompilerParams(vmem_limit_bytes=60<<20),name="sk")(cell,w,adj,ret)
from jax.sharding import PartitionSpec as P
NW=13
def coords():
    a=lax.axis_index("lon"); b=lax.axis_index("lat")
    return a,b
def xk(send,obs_ref,val,inv,mis,ret,recv,recv2,send2,acc,ms,ssem,rsem,ssem2,rsem2):
    a,b=coords()
    me=a*4+b
    yhi=a//16; z=(a//4)%4; x=a%4; y=yhi*2+b//2; core=b%2
    def peer(t,sign):
        u=t//2; dc=t%2
        dx=u%4; dz=(u//4+u)%4; dy=(u//16+u)%4
        py=(y+sign*dy+4)%4; pz=(z+sign*dz+4)%4; px=(x+sign*dx+4)%4; pc=(core+dc)%2
        pa=(py//2)*16+pz*4+px; pb=(py%2)*2+pc
        return pa,pb
    def rc(src,dst,s1,s2,pa,pb):
        return pltpu.make_async_remote_copy(src_ref=src,dst_ref=dst,send_sem=s1,recv_sem=s2,
            device_id={"lon":pa,"lat":pb},device_id_type=pl.DeviceIdType.MESH)
    def snd(t,_):
        pa,pb=peer(t,1)
        rc(send.at[pa*4+pb,pl.ds(0,NW)],recv.at[me,pl.ds(0,NW)],ssem,rsem.at[me],pa,pb).start()
        return 0
    lax.fori_loop(1,128,snd,0)
    recv[me,0:NW]=send[me,0:NW]
    acc[...]=jnp.zeros_like(acc)
    lane=lax.broadcasted_iota(jnp.int32,(16,128),1)
    lw=lane<64
    live=lax.broadcasted_iota(jnp.int32,(16,128),0)<NW
    def wr(t,_):
        pa,pb=peer(t,-1)
        s=pa*4+pb
        rc(send.at[s,pl.ds(0,NW)],recv.at[s,pl.ds(0,NW)],ssem,rsem.at[s],pa,pb).wait_recv()
        return 0
    lax.fori_loop(1,128,wr,0)
    def chunk(c,_):
        o=pl.multiple_of(c*256,256)
        ob=obs_ref[:,pl.ds(o,256)]
        O=(lax.broadcasted_iota(jnp.int32,(512,256),0)==ob).astype(F32).astype(BF)
        xa=[];xb=[]
        for q in range(2):
            m0=jnp.where(live,recv[c*4+2*q],0.0); m1=jnp.where(live,recv[c*4+2*q+1],0.0)
            xa.append(jnp.where(lw,m0,pltpu.roll(m1,64,1)))
            xb.append(jnp.where(lw,pltpu.roll(m0,64,1),m1))
        xx=jnp.concatenate([jnp.concatenate(xa,1),jnp.concatenate(xb,1)],0)
        h=xx.astype(BF).astype(F32); l=xx-h
        L=jnp.concatenate([h,l],0).astype(BF)
        acc[...]+=lax.dot_general(L,O,(((1,),(1,)),((),())),preferred_element_type=F32)
        return 0
    lax.fori_loop(0,32,chunk,0)
    ip=acc[0:32]+acc[32:64]
    ma=inv[0:13]*(ip[0:13]-val[0:13]); mb=inv[13:25]*(ip[16:28]-val[13:25])
    mis[0:13]=ma; mis[13:25]=mb
    ms[...]=jnp.zeros_like(ms)
    ms[0,0:13]=ma; ms[1,0:12]=mb
    def back(c,_):
        o=pl.multiple_of(c*256,256)
        for q in range(2):
            ob=jnp.maximum(obs_ref[:,pl.ds(o+q*128,128)],0)
            ti=jnp.broadcast_to(lax.shift_right_logical(ob,7),(16,128)); li=jnp.broadcast_to(lax.bitwise_and(ob,127),(16,128))
            g=[]
            for h in range(2):
                v=None
                for k in range(4):
                    gk_=jnp.take_along_axis(ms[h,:,k*128:(k+1)*128],li,axis=1,mode="promise_in_bounds")
                    v=gk_ if v is None else jnp.where(ti==k,gk_,v)
                g.append(v)
            va,vb=g
            send2[c*4+2*q]=jnp.where(lw,va,pltpu.roll(vb,64,1))
            send2[c*4+2*q+1]=jnp.where(lw,pltpu.roll(va,64,1),vb)
        return 0
    lax.fori_loop(0,32,back,0)
    def snd2(t,_):
        pa,pb=peer(t,1)
        rc(send2.at[pa*4+pb,pl.ds(0,NW)],recv2.at[me,pl.ds(0,NW)],ssem2,rsem2.at[me],pa,pb).start()
        return 0
    lax.fori_loop(1,128,snd2,0)
    ret[me]=send2[me]
    def wr2(t,_):
        pa,pb=peer(t,-1)
        s=pa*4+pb
        rc(send2.at[s,pl.ds(0,NW)],recv2.at[s,pl.ds(0,NW)],ssem2,rsem2.at[s],pa,pb).wait_recv()
        ret[s,0:NW]=recv2[s,0:NW]
        return 0
    lax.fori_loop(1,128,wr2,0)
    rc(send.at[pl.ds(0,127),pl.ds(0,NW)],recv.at[pl.ds(0,127),pl.ds(0,NW)],ssem,rsem.at[me],a,b).wait_send()
    rc(send2.at[pl.ds(0,127),pl.ds(0,NW)],recv2.at[pl.ds(0,127),pl.ds(0,NW)],ssem2,rsem2.at[me],a,b).wait_send()

def exchange(send,obs,val,inv):
    D=pltpu.SemaphoreType.DMA
    return pl.pallas_call(xk,out_shape=(jax.ShapeDtypeStruct((25,512),F32),jax.ShapeDtypeStruct((128,16,128),F32)),
        in_specs=[VM]*4,out_specs=(VM,VM),
        scratch_shapes=[pltpu.VMEM((128,16,128),F32)]*3+[pltpu.VMEM((64,512),F32),pltpu.VMEM((2,16,512),F32),D,D((128,)),D,D((128,))],
        compiler_params=pltpu.CompilerParams(vmem_limit_bytes=60<<20,has_side_effects=True),name="xk")(send,obs,val,inv)

STEPS = 2


def from_behind(value, axis, steps):
    count = lax.axis_size(axis)
    pairs = [(source, (source + steps) % count) for source in range(count)]
    return lax.ppermute(value, axis, pairs)


def from_behind_2(block, axis, distance):
    devices = range(lax.axis_size(axis))
    route = [(i - distance, i) for i in devices if i - distance in devices]
    return lax.ppermute(block, axis, route)


def padded(cells, sides, width, closed):
    for axis, dim in sides:
        count = lax.axis_size(axis)
        ends = count if closed else count - 1
        head = lax.slice_in_dim(cells, 0, width, axis=dim)
        tail = lax.slice_in_dim(cells, cells.shape[dim] - width, cells.shape[dim], axis=dim)
        cells = jnp.concatenate(
            [
                lax.ppermute(tail, axis, [(i, (i + 1) % count) for i in range(ends)]),
                cells,
                lax.ppermute(head, axis, [((i + 1) % count, i) for i in range(ends)]),
            ],
            axis=dim,
        )
    return cells


def on_device(
    state,
    adjoint_in,
    land_mask,
    east_coef,
    north_coef,
    zonal_flow,
    vertical_coef,
    slot_cell,
    slot_weight,
    arrive_obs,
    obs_value,
    obs_invvar,
):
    levels_n, rows_n, cols_n = state.shape
    msgs = gather(state, slot_cell, slot_weight)
    misfit, ret = exchange(msgs, arrive_obs, obs_value, obs_invvar)
    adjoint_state = scatter(adjoint_in, ret, slot_cell, slot_weight)
    ocean = land_mask.astype(jnp.float32)
    east_weight = east_coef - 0.5 * zonal_flow
    own_east = east_coef + 0.5 * zonal_flow
    west_column = from_behind(east_weight[:, -1:], "lon", 1)
    west_weight = jnp.concatenate([west_column, east_weight[:, :-1]], axis=1)
    south_row = from_behind_2(north_coef[-1:, :], "lat", 1)
    south_weight = jnp.concatenate([south_row, north_coef[:-1, :]], axis=0)
    lat_last = lax.axis_index("lat") == lax.axis_size("lat") - 1
    zero_level = jnp.zeros((1, rows_n, cols_n), jnp.float32)
    for repeat in range(STEPS):
        masked = ocean * adjoint_state
        zonal_pad = padded(masked, (("lon", 2),), 1, True)
        merid_pad = padded(masked, (("lat", 1),), 1, False)
        east_vals = zonal_pad[:, :, 2:]
        west_vals = zonal_pad[:, :, :-2]
        north_vals = merid_pad[:, 2:, :]
        south_vals = merid_pad[:, :-2, :]
        east_diff = masked - east_vals
        north_diff = masked - north_vals
        updated = adjoint_state - own_east * east_diff + west_weight * (west_vals - masked)
        updated = updated - north_coef * north_diff + south_weight * (south_vals - masked)
        fold_top = north_coef[-1][None, :] * masked[:, -1, :]
        lon_n = lax.axis_size("lon")
        mirror = [(i, lon_n - 1 - i) for i in range(lon_n)]
        mirrored = lax.ppermute(fold_top[:, ::-1], "lon", mirror)
        updated = updated.at[:, -1, :].add(jnp.where(lat_last, mirrored, 0.0))
        vertical_term = vertical_coef[None] * (masked[:-1] - masked[1:])
        updated = updated - jnp.concatenate([vertical_term, zero_level], axis=0)
        updated = updated + jnp.concatenate([zero_level, vertical_term], axis=0)
        adjoint_state = updated
    return (adjoint_state, misfit)


def solution(mesh):
    in_specs = (
        P(None, "lat", "lon"),
        P(None, "lat", "lon"),
        P("lat", "lon"),
        P("lat", "lon"),
        P("lat", "lon"),
        P("lat", "lon"),
        P("lat", "lon"),
        P(("lon", "lat"), None),
        P(("lon", "lat"), None),
        P(("lon", "lat"), None),
        P(None, ("lon", "lat")),
        P(None, ("lon", "lat")),
    )
    out_specs = (P(None, "lat", "lon"), P(None, ("lon", "lat")))
    return jax.shard_map(
        on_device, mesh=mesh, in_specs=in_specs, out_specs=out_specs, check_vma=False
    )
```

```python
import jax
import jax.numpy as jnp
from jax import lax
from jax.experimental import pallas as pl
from jax.experimental.pallas import tpu as pltpu
from jax.sharding import PartitionSpec as P

BF = jnp.bfloat16
F32 = jnp.float32
I32 = jnp.int32
NW = 13
NT = (((1,), (1,)), ((), ()))


def iota(shape, dim):
    return lax.broadcasted_iota(I32, shape, dim)


def one_hot(rows, index):
    n = index.shape[1]
    return (iota((rows, n), 0) == index).astype(F32).astype(BF)


def cell_parts(cell):
    row = lax.bitwise_and(lax.shift_right_arithmetic(cell, 7), 63)
    half = lax.shift_left(lax.shift_right_arithmetic(cell, 13), 7)
    return row, lax.bitwise_or(half, lax.bitwise_and(cell, 127))


def remote(src, dst, send_sem, recv_sem, lon, lat):
    return pltpu.make_async_remote_copy(
        src_ref=src,
        dst_ref=dst,
        send_sem=send_sem,
        recv_sem=recv_sem,
        device_id={"lon": lon, "lat": lat},
        device_id_type=pl.DeviceIdType.MESH,
    )


def kernel(
    cell_ref, w_ref, obs_ref, state, adj, mask, east, north, zonal, vert, val, inv,
    out, mis,
    hi, lo, b0, b1, send, recv, acc, ms, back, ret, field, spread, mp, wst, est, wrv, erv,
    coef, ssem, rsem, bsem, tsem, nsem, nrem, hsem, hrem,
):
    a = lax.axis_index("lon")
    b = lax.axis_index("lat")
    me = a * 4 + b
    yhi = a // 16
    z = (a // 4) % 4
    x = a % 4

    def lon_at(j, sign):
        dx = j % 4
        dz = (j // 4 + j) % 4
        dy = (j // 16 + j) % 2
        return ((yhi + dy) % 2) * 16 + ((z + sign * dz + 4) % 4) * 4 + (x + sign * dx + 4) % 4

    def slot(ref, d):
        return ref.at[d, pl.ds(0, NW)]

    def put(src, dst, s1, s2, lon):
        def one(lat):
            remote(slot(src, lon * 4 + lat), slot(dst, me), s1, s2.at[me], lon, lat).start()

        for lat in range(4):
            if lon is a:
                pl.when(b != lat)(lambda: one(lat))
            else:
                one(lat)

    lane = iota((16, 128), 1)
    low = lane < 64
    live = iota((16, 128), 0) < NW

    def pack(va, vb):
        r = low[: va.shape[0]]
        return (
            jnp.where(r, va, pltpu.roll(vb, 64, 1)),
            jnp.where(r, pltpu.roll(va, 64, 1), vb),
        )

    def weights_at(o):
        cell = cell_ref[:, pl.ds(o, 256)]
        w = jnp.where(cell >= 0, w_ref[:, pl.ds(o, 256)], 0.0)
        row, col = cell_parts(cell)
        return w, row, col

    for half in range(2):
        v = state[:, half * 64 : half * 64 + 64, :].reshape(1600, 128)
        h = v.astype(BF)
        hi[:, half * 128 : half * 128 + 128] = h
        lo[:, half * 128 : half * 128 + 128] = (v - h.astype(F32)).astype(BF)

    def gather(lon):
        w, row, col = weights_at(pl.multiple_of(lon * 256, 256))
        cols = one_hot(256, col)
        rows = jnp.where(iota((64, 256), 0) == row, w, 0.0)
        for g in range(5):
            s = slice(g * 320, g * 320 + 320)
            t = jnp.dot(hi[s, :], cols, preferred_element_type=F32)
            t = t + jnp.dot(lo[s, :], cols, preferred_element_type=F32)
            t = t.reshape(5, 8, 8, 256) * rows.reshape(1, 8, 8, 256)
            t = jnp.sum(t, axis=1).reshape(40, 256)
            b0[pl.ds(g * 40, 40), :] = t[:, :128]
            b1[pl.ds(g * 40, 40), :] = t[:, 128:]

        def fold(ref, r0):
            y = ref[pl.ds(r0 * 8, NW, stride=8), :]
            for s in range(1, 8):
                y = y + ref[pl.ds(r0 * 8 + s, NW, stride=8), :]
            return y

        for q, ref in enumerate((b0, b1)):
            m0, m1 = pack(fold(ref, 0), fold(ref, NW))
            send[lon * 4 + 2 * q, 0:NW] = m0
            send[lon * 4 + 2 * q + 1, 0:NW] = m1

    def gather_step(j, _):
        gather(lon_at(j, 1))

        @pl.when(j > 1)
        def _():
            put(send, recv, ssem, rsem, lon_at(j - 1, 1))

        return 0

    lax.fori_loop(1, 32, gather_step, 0)
    gather(a)
    put(send, recv, ssem, rsem, lon_at(31, 1))
    recv[me, 0:NW] = send[me, 0:NW]
    put(send, recv, ssem, rsem, a)

    def take(src, dst, s1, s2, lon):
        def one(lat):
            remote(slot(src, lon * 4 + lat), slot(dst, lon * 4 + lat), s1, s2.at[lon * 4 + lat], lon, lat).wait_recv()

        for lat in range(4):
            if lon is a:
                pl.when(b != lat)(lambda: one(lat))
            else:
                one(lat)

    def unpack(ref, lon):
        xa = []
        xb = []
        for q in range(2):
            m0 = jnp.where(live, ref[lon * 4 + 2 * q], 0.0)
            m1 = jnp.where(live, ref[lon * 4 + 2 * q + 1], 0.0)
            va, vb = pack(m0, m1)
            xa.append(va)
            xb.append(vb)
        return jnp.concatenate(xa, 1), jnp.concatenate(xb, 1)

    acc[...] = jnp.zeros_like(acc)

    def observe(lon):
        ob = obs_ref[:, pl.ds(pl.multiple_of(lon * 256, 256), 256)]
        xx = jnp.concatenate(unpack(recv, lon), 0)
        h = xx.astype(BF).astype(F32)
        parts = jnp.concatenate([h, xx - h], 0).astype(BF)
        acc[...] += lax.dot_general(parts, one_hot(512, ob), NT, preferred_element_type=F32)

    def observe_step(j, _):
        lon = lon_at(j, -1)
        take(send, recv, ssem, rsem, lon)
        observe(lon)
        return 0

    lax.fori_loop(1, 32, observe_step, 0)
    take(send, recv, ssem, rsem, a)
    observe(a)
    ip = acc[0:32] + acc[32:64]
    ma = inv[0:13] * (ip[0:13] - val[0:13])
    mb = inv[13:25] * (ip[16:28] - val[13:25])
    mis[0:13] = ma
    mis[13:25] = mb
    ms[...] = jnp.zeros_like(ms)
    ms[0, 0:13] = ma
    ms[1, 0:12] = mb

    def answer(lon):
        for q in range(2):
            o = pl.multiple_of(lon * 256 + q * 128, 128)
            ob = jnp.maximum(obs_ref[:, pl.ds(o, 128)], 0)
            tile = jnp.broadcast_to(lax.shift_right_logical(ob, 7), (16, 128))
            at = jnp.broadcast_to(lax.bitwise_and(ob, 127), (16, 128))
            g = []
            for h in range(2):
                v = None
                for k in range(4):
                    u = jnp.take_along_axis(
                        ms[h, :, k * 128 : k * 128 + 128], at, axis=1, mode="promise_in_bounds"
                    )
                    v = u if v is None else jnp.where(tile == k, u, v)
                g.append(v)
            m0, m1 = pack(g[0], g[1])
            back[lon * 4 + 2 * q] = m0
            back[lon * 4 + 2 * q + 1] = m1

    def answer_step(j, _):
        answer(lon_at(j, 1))

        @pl.when(j > 1)
        def _():
            put(back, ret, bsem, tsem, lon_at(j - 1, 1))

        return 0

    lax.fori_loop(1, 32, answer_step, 0)
    answer(a)
    put(back, ret, bsem, tsem, lon_at(31, 1))
    ret[me] = back[me]
    put(back, ret, bsem, tsem, a)

    for half in range(2):
        field[:, half * 128 : half * 128 + 128] = adj[:, half * 64 : half * 64 + 64, :].reshape(1600, 128)

    def scatter(lon):
        w, row, col = weights_at(pl.multiple_of(lon * 256, 256))
        cols = one_hot(256, col)
        rows = one_hot(64, row)
        xa, xb = unpack(ret, lon)
        xa = xa * w
        xb = xb * w
        xah = xa.astype(BF).astype(F32)
        xbh = xb.astype(BF).astype(F32)
        for l in range(25):
            n = l if l < NW else l - NW
            for k, y in enumerate((xah, xa - xah) if l < NW else (xbh, xb - xbh)):
                spread[l * 64 : l * 64 + 64, k * 256 : k * 256 + 256] = (
                    rows * jnp.broadcast_to(y[n : n + 1], (64, 256)).astype(BF)
                )
        both = jnp.concatenate([cols, cols], 1)
        for g in range(5):
            s = slice(g * 320, g * 320 + 320)
            field[s, :] += lax.dot_general(spread[s, :], both, NT, preferred_element_type=F32)

    def scatter_step(j, _):
        lon = lon_at(j, -1)
        take(back, ret, bsem, tsem, lon)
        scatter(lon)
        return 0

    lax.fori_loop(1, 32, scatter_step, 0)
    take(back, ret, bsem, tsem, a)
    scatter(a)
    for half in range(2):
        out[:, half * 64 : half * 64 + 64, :] = field[:, half * 128 : half * 128 + 128].reshape(25, 64, 128)

    ocean = mask[...].astype(F32)
    own_e = east[...] + 0.5 * zonal[...]
    mp[0, 25, 8:136, :] = north[...]
    mp[0, 26, 8:136, :] = east[...] - 0.5 * zonal[...]
    last = b == 3

    @pl.when(b == 0)
    def _():
        mp[:, :, 7:8, :] = jnp.zeros((2, 27, 1, 128), F32)

    mirror = 127 - iota((32, 128), 1)
    wlane = iota((32, 128), 1)
    lane_r = iota((128, 128), 1)
    row_r = iota((128, 128), 0)
    w_lon = (a // 16) * 16 + a % 16
    west = (a + 31) % 32
    eastn = (a + 1) % 32

    for s in range(2):
        def stage(l, carry):
            wp, ep = carry
            m = mp[s, l, 8:136, :]
            for g in range(4):
                rows_g = m[g * 32 : g * 32 + 32]
                k = g * 32 + l
                wp = jnp.where(wlane == k, pltpu.roll(rows_g, (k + 1) % 128, 1), wp)
                ep = jnp.where(wlane == k, pltpu.roll(rows_g, k, 1), ep)
            return wp, ep

        def masked(l, _):
            mp[s, l, 8:136, :] = ocean * out[l]
            return 0

        lax.fori_loop(0, 25, masked, 0)
        n_lev = 27 if s == 0 else 25
        zero = jnp.zeros((32, 128), F32)
        wp, ep = lax.fori_loop(0, n_lev, stage, (zero, zero))
        wst[s] = wp
        est[s] = ep
        n_row = 26 if s == 0 else 25
        up = remote(mp.at[s, pl.ds(0, n_row), 135, :], mp.at[s, pl.ds(0, n_row), 7, :], nsem.at[s, 0], nrem.at[s, 0], a, b + 1)
        up_in = remote(mp.at[s, pl.ds(0, n_row), 135, :], mp.at[s, pl.ds(0, n_row), 7, :], nsem.at[s, 0], nrem.at[s, 0], a, b - 1)
        down = remote(mp.at[s, pl.ds(0, 25), 8, :], mp.at[s, pl.ds(0, 25), 136, :], nsem.at[s, 1], nrem.at[s, 1], a, b - 1)
        down_in = remote(mp.at[s, pl.ds(0, 25), 8, :], mp.at[s, pl.ds(0, 25), 136, :], nsem.at[s, 1], nrem.at[s, 1], a, b + 1)
        to_e = remote(wst.at[s], wrv.at[s], hsem.at[s, 0], hrem.at[s, 0], eastn, b)
        to_w = remote(est.at[s], erv.at[s], hsem.at[s, 1], hrem.at[s, 1], west, b)
        over = remote(coef.at[s, pl.ds(0, 25)], mp.at[s, pl.ds(0, 25), 136, :], nsem.at[s, 2], nrem.at[s, 2], 31 - a, b)

        @pl.when(last)
        def _():
            for l in range(25):
                coef[s, l : l + 1, :] = north[127:128, :] * mp[s, l, 135:136, :]
            coef[s] = jnp.take_along_axis(coef[s], mirror, axis=1, mode="promise_in_bounds")

        pl.when(b < 3)(lambda: up.start())
        pl.when(b > 0)(lambda: down.start())
        to_e.start()
        to_w.start()
        pl.when(last)(lambda: over.start())

        pl.when(b > 0)(lambda: up_in.wait_recv())
        pl.when(b < 3)(lambda: down_in.wait_recv())
        pl.when(last)(lambda: over.wait_recv())
        to_e.wait_recv()
        to_w.wait_recv()

        def west_of(l, m):
            return jnp.where(lane_r == 0, halo(wrv[s], l, 0), pltpu.roll(m, 1, 1))

        def east_of(l, m):
            return jnp.where(lane_r == 127, halo(erv[s], l, 1), pltpu.roll(m, 127, 1))

        def halo(h, l, shift):
            return jnp.concatenate(
                [pltpu.roll(h, (128 - shift - (g * 32 + l)) % 128, 1) for g in range(4)], 0
            )

        if s == 0:
            south_w = mp[0, 25, 7:135, :]
            west_w = west_of(26, mp[0, 26, 8:136, :])
            diag = own_e + west_w + north[...] + south_w
            north_w = jnp.where(jnp.logical_and(row_r == 127, last), 1.0, north[...])

        def step(l, _):
            m = mp[s, l, 8:136, :]
            above = jnp.where(l < 24, 1.0, 0.0)
            below = jnp.where(l > 0, 1.0, 0.0)
            v = out[l] - diag * m
            v = v + own_e * east_of(l, m) + west_w * west_of(l, m)
            v = v + north_w * mp[s, l, 9:137, :] + south_w * mp[s, l, 7:135, :]
            up_l = mp[s, jnp.minimum(l + 1, 24), 8:136, :]
            dn_l = mp[s, jnp.maximum(l - 1, 0), 8:136, :]
            v = v + vert[...] * (above * (up_l - m) + below * (dn_l - m))
            out[l] = v
            return 0

        lax.fori_loop(0, 25, step, 0)
        pl.when(b < 3)(lambda: up.wait_send())
        pl.when(b > 0)(lambda: down.wait_send())
        to_e.wait_send()
        to_w.wait_send()
        pl.when(last)(lambda: over.wait_send())

    many = pl.ds(0, 127)
    remote(send.at[many, pl.ds(0, NW)], recv.at[many, pl.ds(0, NW)], ssem, rsem.at[me], a, b).wait_send()
    remote(back.at[many, pl.ds(0, NW)], ret.at[many, pl.ds(0, NW)], bsem, tsem.at[me], a, b).wait_send()


def on_device(
    state, adjoint_in, land_mask, east_coef, north_coef, zonal_flow, vertical_coef,
    slot_cell, slot_weight, arrive_obs, obs_value, obs_invvar,
):
    dma = pltpu.SemaphoreType.DMA
    vm = pl.BlockSpec(memory_space=pltpu.VMEM)
    messages = pltpu.VMEM((128, 16, 128), F32)
    edge = pltpu.VMEM((2, 32, 128), F32)
    return pl.pallas_call(
        kernel,
        out_shape=(
            jax.ShapeDtypeStruct((25, 128, 128), F32),
            jax.ShapeDtypeStruct((25, 512), F32),
        ),
        in_specs=[vm] * 12,
        out_specs=(vm, vm),
        scratch_shapes=[
            pltpu.VMEM((1600, 256), BF),
            pltpu.VMEM((1600, 256), BF),
            pltpu.VMEM((208, 128), F32),
            pltpu.VMEM((208, 128), F32),
            messages,
            messages,
            pltpu.VMEM((64, 512), F32),
            pltpu.VMEM((2, 16, 512), F32),
            messages,
            messages,
            pltpu.VMEM((1600, 256), F32),
            pltpu.VMEM((1600, 512), BF),
            pltpu.VMEM((2, 27, 144, 128), F32),
            edge,
            edge,
            edge,
            edge,
            edge,
            dma,
            dma((128,)),
            dma,
            dma((128,)),
            dma((2, 3)),
            dma((2, 3)),
            dma((2, 2)),
            dma((2, 2)),
        ],
        compiler_params=pltpu.CompilerParams(vmem_limit_bytes=60 << 20, has_side_effects=True),
        name="adjoint",
    )(
        slot_cell, slot_weight, arrive_obs, state, adjoint_in, land_mask, east_coef, north_coef,
        zonal_flow, vertical_coef, obs_value, obs_invvar,
    )


def solution(mesh):
    grid = P("lat", "lon")
    cube = P(None, "lat", "lon")
    slots = P(("lon", "lat"), None)
    obs = P(None, ("lon", "lat"))
    return jax.shard_map(
        on_device,
        mesh=mesh,
        in_specs=(cube, cube, grid, grid, grid, grid, grid, slots, slots, slots, obs, obs),
        out_specs=(cube, obs),
        check_vma=False,
    )
```

```python
import jax
import jax.numpy as jnp
from jax import lax
from jax.experimental import pallas as pl
from jax.experimental.pallas import tpu as pltpu
from jax.sharding import PartitionSpec as P

BF = jnp.bfloat16
F32 = jnp.float32
I32 = jnp.int32
NW = 13
LEAD = 10
NT = (((1,), (1,)), ((), ()))


def iota(shape, dim):
    return lax.broadcasted_iota(I32, shape, dim)


def one_hot(rows, index):
    n = index.shape[1]
    return (iota((rows, n), 0) == index).astype(F32).astype(BF)


def cell_parts(cell):
    row = lax.bitwise_and(lax.shift_right_arithmetic(cell, 7), 63)
    half = lax.shift_left(lax.shift_right_arithmetic(cell, 13), 7)
    return row, lax.bitwise_or(half, lax.bitwise_and(cell, 127))


def remote(src, dst, send_sem, recv_sem, lon, lat):
    return pltpu.make_async_remote_copy(
        src_ref=src,
        dst_ref=dst,
        send_sem=send_sem,
        recv_sem=recv_sem,
        device_id={"lon": lon, "lat": lat},
        device_id_type=pl.DeviceIdType.MESH,
    )


def kernel(
    cell_ref, w_ref, obs_ref, state, adj_hbm, mask, east, north, zonal, vert, val, inv,
    out, mis,
    hi, lo, b0, b1, send, recv, acc, ms, back, ret, field, spread, mp, adj, u, cf, ed,
    pp, ppw, ppe, rn, rs, nh, sh, fd, cst, crv, nst, nrv,
    ssem, rsem, bsem, tsem, nsem, nrem, hsem, hrem, csem, crem, lsem,
):
    a = lax.axis_index("lon")
    b = lax.axis_index("lat")
    me = a * 4 + b
    yhi = lax.div(a, 16)
    z = lax.rem(lax.div(a, 4), 4)
    x = lax.rem(a, 4)

    def lon_at(j, sign):
        dx = lax.rem(j, 4)
        dz = lax.rem(lax.div(j, 4) + j, 4)
        dy = lax.rem(lax.div(j, 16) + j + yhi, 2)
        return dy * 16 + lax.rem(z + sign * dz + 4, 4) * 4 + lax.rem(x + sign * dx + 4, 4)

    barrier = pltpu.get_barrier_semaphore()

    def hello(t, _):
        d = lax.rem(me + t, 128)
        pl.semaphore_signal(
            barrier,
            inc=1,
            device_id={"lon": lax.div(d, 4), "lat": lax.rem(d, 4)},
            device_id_type=pl.DeviceIdType.MESH,
        )
        return 0

    lax.fori_loop(1, 128, hello, 0)
    load = pltpu.make_async_copy(adj_hbm, adj, lsem)
    load.start()

    def slot(ref, d):
        return ref.at[d, pl.ds(0, NW)]

    def put(src, dst, s1, s2, lon):
        def one(lat):
            remote(slot(src, lon * 4 + lat), slot(dst, me), s1, s2.at[me], lon, lat).start()

        for lat in range(4):
            if lon is a:
                pl.when(b != lat)(lambda: one(lat))
            else:
                one(lat)

    lane = iota((16, 128), 1)
    low = lane < 64
    live = iota((16, 128), 0) < NW

    def pack(va, vb):
        r = low[: va.shape[0]]
        return (
            jnp.where(r, va, pltpu.roll(vb, 64, 1)),
            jnp.where(r, pltpu.roll(va, 64, 1), vb),
        )

    def weights_at(o):
        cell = cell_ref[:, pl.ds(o, 256)]
        w = jnp.where(cell >= 0, w_ref[:, pl.ds(o, 256)], 0.0)
        row, col = cell_parts(cell)
        return w, row, col

    for half in range(2):
        v = state[:, half * 64 : half * 64 + 64, :].reshape(1600, 128)
        h = v.astype(BF)
        hi[:, half * 128 : half * 128 + 128] = h
        lo[:, half * 128 : half * 128 + 128] = (v - h.astype(F32)).astype(BF)

    def gather(lon):
        w, row, col = weights_at(pl.multiple_of(lon * 256, 256))
        cols = one_hot(256, col)
        rows = jnp.where(iota((64, 256), 0) == row, w, 0.0)
        for g in range(5):
            s = slice(g * 320, g * 320 + 320)
            t = jnp.dot(hi[s, :], cols, preferred_element_type=F32)
            t = t + jnp.dot(lo[s, :], cols, preferred_element_type=F32)
            t = t.reshape(5, 8, 8, 256) * rows.reshape(1, 8, 8, 256)
            t = jnp.sum(t, axis=1).reshape(40, 256)
            b0[pl.ds(g * 40, 40), :] = t[:, :128]
            b1[pl.ds(g * 40, 40), :] = t[:, 128:]

        def fold(ref, r0):
            y = ref[pl.ds(r0 * 8, NW, stride=8), :]
            for s in range(1, 8):
                y = y + ref[pl.ds(r0 * 8 + s, NW, stride=8), :]
            return y

        for q, ref in enumerate((b0, b1)):
            m0, m1 = pack(fold(ref, 0), fold(ref, NW))
            send[lon * 4 + 2 * q, 0:NW] = m0
            send[lon * 4 + 2 * q + 1, 0:NW] = m1

    def take(src, dst, s1, s2, lon):
        def one(lat):
            remote(slot(src, lon * 4 + lat), slot(dst, lon * 4 + lat), s1, s2.at[lon * 4 + lat], lon, lat).wait_recv()

        for lat in range(4):
            if lon is a:
                pl.when(b != lat)(lambda: one(lat))
            else:
                one(lat)

    def unpack(ref, lon):
        xa = []
        xb = []
        for q in range(2):
            m0 = jnp.where(live, ref[lon * 4 + 2 * q], 0.0)
            m1 = jnp.where(live, ref[lon * 4 + 2 * q + 1], 0.0)
            va, vb = pack(m0, m1)
            xa.append(va)
            xb.append(vb)
        return jnp.concatenate(xa, 1), jnp.concatenate(xb, 1)

    last = b == 3
    eastn = lax.rem(a + 1, 32)
    westn = lax.rem(a + 31, 32)
    lane_h = iota((64, 128), 1)
    even = lax.rem(lane_h, 2) == 0
    csend = remote(cst, crv, csem.at[0], crem.at[0], eastn, b)
    nsend = remote(nst, nrv, csem.at[1], crem.at[1], a, b + 1)

    def coefs_out():
        csend.start()
        pl.when(b < 3)(lambda: nsend.start())

    weight = east[...] - 0.5 * zonal[...]
    cst[...] = jnp.where(
        lane_h < 64, pltpu.roll(weight[0:64], 1, 1), pltpu.roll(weight[64:128], 65, 1)
    )
    nst[...] = jnp.broadcast_to(north[127:128, :], (8, 128))

    @pl.when(b == 0)
    def _():
        nrv[...] = jnp.zeros_like(nrv)
        sh[...] = jnp.zeros_like(sh)

    for s in range(2):
        mp[s, pl.ds(7, 25, stride=144), :] = jnp.zeros((25, 128), F32)
        mp[s, pl.ds(136, 25, stride=144), :] = jnp.zeros((25, 128), F32)

    acc[...] = jnp.zeros_like(acc)

    def observe(lon):
        ob = obs_ref[:, pl.ds(pl.multiple_of(lon * 256, 256), 256)]
        xx = jnp.concatenate(unpack(recv, lon), 0)
        h = xx.astype(BF).astype(F32)
        parts = jnp.concatenate([h, xx - h], 0).astype(BF)
        acc[...] += lax.dot_general(parts, one_hot(512, ob), NT, preferred_element_type=F32)

    def gather_only(j, _):
        gather(lon_at(j, 1))
        return 0

    lax.fori_loop(1, LEAD + 1, gather_only, 0)
    pl.semaphore_wait(barrier, 127)
    coefs_out()

    def burst(j, _):
        put(send, recv, ssem, rsem, lon_at(j, 1))
        return 0

    lax.fori_loop(1, LEAD, burst, 0)

    def gather_step(j, _):
        put(send, recv, ssem, rsem, lon_at(j - 1, 1))
        lon = lon_at(j - LEAD, -1)
        take(send, recv, ssem, rsem, lon)
        gather(lon_at(j, 1))
        observe(lon)
        return 0

    lax.fori_loop(LEAD + 1, 32, gather_step, 0)
    put(send, recv, ssem, rsem, lon_at(31, 1))
    gather(a)
    recv[me, 0:NW] = send[me, 0:NW]

    def observe_step(j, _):
        lon = lon_at(j, -1)
        take(send, recv, ssem, rsem, lon)
        observe(lon)
        return 0

    put(send, recv, ssem, rsem, a)
    lax.fori_loop(32 - LEAD, 32, observe_step, 0)
    take(send, recv, ssem, rsem, a)
    observe(a)
    ip = acc[0:32] + acc[32:64]
    ma = inv[0:13] * (ip[0:13] - val[0:13])
    mb = inv[13:25] * (ip[16:28] - val[13:25])
    mis[0:13] = ma
    mis[13:25] = mb
    ms[...] = jnp.zeros_like(ms)
    ms[0, 0:13] = ma
    ms[1, 0:12] = mb

    def answer(lon):
        for q in range(2):
            o = pl.multiple_of(lon * 256 + q * 128, 128)
            ob = jnp.maximum(obs_ref[:, pl.ds(o, 128)], 0)
            tile = jnp.broadcast_to(lax.shift_right_logical(ob, 7), (16, 128))
            at = jnp.broadcast_to(lax.bitwise_and(ob, 127), (16, 128))
            g = []
            for h in range(2):
                v = None
                for k in range(4):
                    u = jnp.take_along_axis(
                        ms[h, :, k * 128 : k * 128 + 128], at, axis=1, mode="promise_in_bounds"
                    )
                    v = u if v is None else jnp.where(tile == k, u, v)
                g.append(v)
            m0, m1 = pack(g[0], g[1])
            back[lon * 4 + 2 * q] = m0
            back[lon * 4 + 2 * q + 1] = m1

    answer(lon_at(1, 1))
    answer(lon_at(2, 1))

    def answer_step(i, _):
        j = 2 * i
        put(back, ret, bsem, tsem, lon_at(j - 1, 1))
        put(back, ret, bsem, tsem, lon_at(j, 1))
        answer(lon_at(j + 1, 1))
        answer(lon_at(j + 2, 1))
        return 0

    lax.fori_loop(1, 15, answer_step, 0)
    put(back, ret, bsem, tsem, lon_at(29, 1))
    put(back, ret, bsem, tsem, lon_at(30, 1))
    answer(lon_at(31, 1))
    answer(a)
    put(back, ret, bsem, tsem, lon_at(31, 1))
    ret[me] = back[me]
    put(back, ret, bsem, tsem, a)
    load.wait()

    for half in range(2):
        field[:, half * 128 : half * 128 + 128] = adj[:, half * 64 : half * 64 + 64, :].reshape(1600, 128)

    def scatter(lon):
        w, row, col = weights_at(pl.multiple_of(lon * 256, 256))
        cols = one_hot(256, col)
        rows = one_hot(64, row)
        xa, xb = unpack(ret, lon)
        xa = xa * w
        xb = xb * w
        xah = xa.astype(BF).astype(F32)
        xbh = xb.astype(BF).astype(F32)
        for l in range(25):
            n = l if l < NW else l - NW
            for k, y in enumerate((xah, xa - xah) if l < NW else (xbh, xb - xbh)):
                spread[l * 64 : l * 64 + 64, k * 256 : k * 256 + 256] = (
                    rows * jnp.broadcast_to(y[n : n + 1], (64, 256)).astype(BF)
                )
        both = jnp.concatenate([cols, cols], 1)
        for g in range(5):
            s = slice(g * 320, g * 320 + 320)
            field[s, :] += lax.dot_general(spread[s, :], both, NT, preferred_element_type=F32)

    def scatter_step(j, _):
        lon = lon_at(j, -1)
        take(back, ret, bsem, tsem, lon)
        scatter(lon)
        return 0

    lax.fori_loop(1, 32, scatter_step, 0)
    take(back, ret, bsem, tsem, a)
    scatter(a)
    csend.wait_recv()
    pl.when(b > 0)(lambda: nsend.wait_recv())
    lane_r = iota((128, 128), 1)
    row_r = iota((128, 128), 0)
    own_e = east[...] + 0.5 * zonal[...]
    halo_w = jnp.concatenate([crv[...], pltpu.roll(crv[...], 64, 1)], 0)
    west_w = jnp.where(lane_r == 0, halo_w, pltpu.roll(weight, 1, 1))
    south_w = jnp.where(row_r == 0, nrv[0:1, :], pltpu.roll(north[...], 1, 0))
    cf[0] = own_e + west_w + north[...] + south_w + 2.0 * vert[...]
    cf[1] = jnp.where(lane_r == 127, 0.0, own_e)
    cf[2] = jnp.where(lane_r == 0, 0.0, west_w)
    cf[3] = south_w
    cf[4] = mask[...].astype(F32)
    south_0 = south_w[0:1, :]
    north_127 = jnp.where(last, 1.0, north[127:128, :])
    for g in range(2):
        r = slice(g * 64, g * 64 + 64)
        edge = jnp.where(
            even,
            jnp.broadcast_to(west_w[r, 0:1], (64, 128)),
            jnp.broadcast_to(own_e[r, 127:128], (64, 128)),
        )
        cf[5, r, :] = edge
    mirror = 127 - iota((25, 128), 1)

    for s in range(2):
        to_n = remote(rn.at[s], sh.at[s], nsem.at[s, 0], nrem.at[s, 0], a, b + 1)
        to_s = remote(rs.at[s], nh.at[s], nsem.at[s, 1], nrem.at[s, 1], a, b - 1)
        over = remote(fd.at[s], nh.at[s], nsem.at[s, 2], nrem.at[s, 2], 31 - a, b)
        to_e = remote(pp.at[s], ppw.at[s], hsem.at[s, 0], hrem.at[s, 0], eastn, b)
        to_w = remote(pp.at[s], ppe.at[s], hsem.at[s, 1], hrem.at[s, 1], westn, b)
        packed = [jnp.zeros((64, 128), F32)] * 2
        for l in range(25):
            if s == 0:
                v = jnp.concatenate(
                    [field[l * 64 : l * 64 + 64, 0:128], field[l * 64 : l * 64 + 64, 128:256]], 0
                )
            else:
                v = u[l * 128 : l * 128 + 128, :] + edges(0, l)
            u[l * 128 : l * 128 + 128, :] = v
            m = cf[4] * v
            mp[s, l * 144 + 8 : l * 144 + 136, :] = m
            for g in range(2):
                k = g * 64 + 2 * l
                sel = (lane_h == k) | (lane_h == (k + 127) % 128)
                packed[g] = jnp.where(sel, pltpu.roll(m[g * 64 : g * 64 + 64], k, 1), packed[g])
        top = mp[s, pl.ds(135, 25, stride=144), :]
        rn[s, 0:25] = top
        rs[s, 0:25] = mp[s, pl.ds(8, 25, stride=144), :]
        fd[s, 0:25] = jnp.take_along_axis(
            north[127:128, :] * top, mirror, axis=1, mode="promise_in_bounds"
        )
        pp[s] = jnp.where(lane_h == 127, packed[0], jnp.where(lane_h < 63, packed[0], packed[1]))

        pl.when(b < 3)(lambda: to_n.start())
        pl.when(b > 0)(lambda: to_s.start())
        pl.when(last)(lambda: over.start())
        to_e.start()
        to_w.start()

        def step(l, _):
            base = pl.multiple_of(l * 144, 8)
            m = mp[s, pl.ds(base + 8, 128), :]
            at = pl.ds(pl.multiple_of(l * 128, 8), 128)
            v = u[at, :] - cf[0] * m
            v = v + cf[1] * pltpu.roll(m, 127, 1) + cf[2] * pltpu.roll(m, 1, 1)
            v = v + north[...] * mp[s, pl.ds(base + 9, 128), :]
            v = v + cf[3] * mp[s, pl.ds(base + 7, 128), :]
            hi_l = pl.multiple_of(jnp.minimum(l + 1, 24) * 144, 8)
            lo_l = pl.multiple_of(jnp.maximum(l - 1, 0) * 144, 8)
            v = v + vert[...] * (mp[s, pl.ds(hi_l + 8, 128), :] + mp[s, pl.ds(lo_l + 8, 128), :])
            u[at, :] = v
            return 0

        lax.fori_loop(0, 25, step, 0)
        pl.when(b > 0)(lambda: to_n.wait_recv())
        pl.when(b < 3)(lambda: to_s.wait_recv())
        pl.when(last)(lambda: over.wait_recv())
        to_e.wait_recv()
        to_w.wait_recv()
        u[pl.ds(127, 25, stride=128), :] += north_127 * nh[s, 0:25]
        u[pl.ds(0, 25, stride=128), :] += south_0 * sh[s, 0:25]
        wide = jnp.where(even, pltpu.roll(ppw[s], 1, 1), pltpu.roll(ppe[s], 127, 1))
        ed[s, 0:64, :] = wide * cf[5, 0:64, :]
        ed[s, 64:128, :] = wide * cf[5, 64:128, :]

        def edges(s, l):
            y = jnp.concatenate(
                [
                    pltpu.roll(ed[s, g * 64 : g * 64 + 64, :], (128 - g * 64 - 2 * l) % 128, 1)
                    for g in range(2)
                ],
                0,
            )
            return jnp.where((lane_r == 0) | (lane_r == 127), y, 0.0)

        pl.when(b < 3)(lambda: to_n.wait_send())
        pl.when(b > 0)(lambda: to_s.wait_send())
        pl.when(last)(lambda: over.wait_send())
        to_e.wait_send()
        to_w.wait_send()

    for l in range(25):
        out[l] = u[l * 128 : l * 128 + 128, :] + edges(1, l)
    csend.wait_send()
    pl.when(b < 3)(lambda: nsend.wait_send())
    many = pl.ds(0, 127)
    remote(send.at[many, pl.ds(0, NW)], recv.at[many, pl.ds(0, NW)], ssem, rsem.at[me], a, b).wait_send()
    remote(back.at[many, pl.ds(0, NW)], ret.at[many, pl.ds(0, NW)], bsem, tsem.at[me], a, b).wait_send()


def on_device(
    state, adjoint_in, land_mask, east_coef, north_coef, zonal_flow, vertical_coef,
    slot_cell, slot_weight, arrive_obs, obs_value, obs_invvar,
):
    dma = pltpu.SemaphoreType.DMA
    vm = pl.BlockSpec(memory_space=pltpu.VMEM)
    messages = pltpu.VMEM((128, 16, 128), F32)
    columns = pltpu.VMEM((2, 64, 128), F32)
    rows = pltpu.VMEM((2, 32, 128), F32)
    return pl.pallas_call(
        kernel,
        out_shape=(
            jax.ShapeDtypeStruct((25, 128, 128), F32),
            jax.ShapeDtypeStruct((25, 512), F32),
        ),
        in_specs=[vm] * 4 + [pl.BlockSpec(memory_space=pl.ANY)] + [vm] * 7,
        out_specs=(vm, vm),
        scratch_shapes=[
            pltpu.VMEM((1600, 256), BF),
            pltpu.VMEM((1600, 256), BF),
            pltpu.VMEM((208, 128), F32),
            pltpu.VMEM((208, 128), F32),
            messages,
            messages,
            pltpu.VMEM((64, 512), F32),
            pltpu.VMEM((2, 16, 512), F32),
            messages,
            messages,
            pltpu.VMEM((1600, 256), F32),
            pltpu.VMEM((1600, 512), BF),
            pltpu.VMEM((2, 3600, 128), F32),
            pltpu.VMEM((25, 128, 128), F32),
            pltpu.VMEM((3200, 128), F32),
            pltpu.VMEM((6, 128, 128), F32),
            pltpu.VMEM((2, 128, 128), F32),
            columns,
            columns,
            columns,
            rows,
            rows,
            rows,
            rows,
            rows,
            pltpu.VMEM((64, 128), F32),
            pltpu.VMEM((64, 128), F32),
            pltpu.VMEM((8, 128), F32),
            pltpu.VMEM((8, 128), F32),
            dma,
            dma((128,)),
            dma,
            dma((128,)),
            dma((2, 3)),
            dma((2, 3)),
            dma((2, 2)),
            dma((2, 2)),
            dma((2,)),
            dma((2,)),
            dma,
        ],
        compiler_params=pltpu.CompilerParams(vmem_limit_bytes=60 << 20, has_side_effects=True, collective_id=0),
        name="adjoint",
    )(
        slot_cell, slot_weight, arrive_obs, state, adjoint_in, land_mask, east_coef, north_coef,
        zonal_flow, vertical_coef, obs_value, obs_invvar,
    )


def solution(mesh):
    grid = P("lat", "lon")
    cube = P(None, "lat", "lon")
    slots = P(("lon", "lat"), None)
    obs = P(None, ("lon", "lat"))
    return jax.shard_map(
        on_device,
        mesh=mesh,
        in_specs=(cube, cube, grid, grid, grid, grid, grid, slots, slots, slots, obs, obs),
        out_specs=(cube, obs),
        check_vma=False,
    )
```
